32 devices in a mesh: img: 2 (over x), gy: 4 (over z), gx: 4 (over y, core).
Axes of the slice: x: 2, y: 2, z: 4, core: 2. Of those that a mesh axis runs over, the one named last changes fastest.
Arguments:
- latent: float32 [4, 64, 64, 4], P('img', 'gy', 'gx'), may hold values from -6 to 6
- noise: float32 [4, 64, 64, 4], P('img', 'gy', 'gx'), may hold values from -6 to 6
- timesteps: int32 [4], P('img'), may hold values from 0 to 999, as said below
- condition: bfloat16 [4, 32, 32, 1152], P('img', 'gy', 'gx'), may hold values from -6 to 6
- embed_weight: float32 [16, 1152], replicated, may hold values from -1.5 to 1.5
- embed_bias: float32 [1152], replicated, may hold values from -3 to 3
- modulation: bfloat16 [1152, 6912], P(('gy', 'gx')), may hold values from -0.1875 to 0.1875
- modulation_bias: float32 [6912], replicated, may hold values from -2 to 2
- project_in: bfloat16 [1152, 3456], P(('gy', 'gx')), may hold values from -0.1875 to 0.1875
- project_out: bfloat16 [1152, 1152], P(('gy', 'gx')), may hold values from -1.5 to 1.5
- gate_up: bfloat16 [1152, 6144], P(('gy', 'gx')), may hold values from -0.1875 to 0.1875
- down_weight: bfloat16 [3072, 1152], P(('gy', 'gx')), may hold values from -0.109375 to 0.109375
- final_modulation: bfloat16 [1152, 2304], P(('gy', 'gx')), may hold values from -0.1875 to 0.1875
- final_offsets: float32 [2304], replicated, may hold values from -2 to 2
- final_weight: float32 [1152, 16], replicated, may hold values from -0.1875 to 0.1875
- final_bias: float32 [16], replicated, may hold values from -2 to 2
- cotangent: float32 [4, 64, 64, 4], P('img', 'gy', 'gx'), may hold values from -6 to 6
Outputs:
- prediction: float32 [4, 64, 64, 4], P('img', 'gy', 'gx')
- latent_grad: float32 [4, 64, 64, 4], P('img', 'gy', 'gx')
- condition_grad: float32 [4, 32, 32, 1152], P('img', 'gy', 'gx')
- embed_weight_grad: float32 [16, 1152], replicated
- embed_bias_grad: float32 [1152], replicated
- modulation_grad: float32 [1152, 6912], P(('gy', 'gx'))
- modulation_bias_grad: float32 [6912], replicated
- project_in_grad: float32 [1152, 3456], P(('gy', 'gx'))
- project_out_grad: float32 [1152, 1152], P(('gy', 'gx'))
- gate_up_grad: float32 [1152, 6144], P(('gy', 'gx'))
- down_weight_grad: float32 [3072, 1152], P(('gy', 'gx'))
- final_modulation_grad: float32 [1152, 2304], P(('gy', 'gx'))
- final_offsets_grad: float32 [2304], replicated
- final_weight_grad: float32 [1152, 16], replicated
- final_bias_grad: float32 [16], replicated
The draws below stay inside these ranges and needn't reach their ends.
Inputs may be any that keep to these rules, and one draw needn't show every extreme that they name: `timesteps`: timestep index of each image, out of 1000 steps; in every draw some image has index 0 and another has index 999.
All inputs are finite; a program needn't handle non-finite values.
Results may differ from the reference program's by a relative error of at most 0.022.
Values may be sent and summed in bfloat16 or wider, within the bound.
A program may use at most 320 MiB of HBM per device.

```python
import math
import jax
import jax.numpy as jnp
from jax import lax

D = 1152
HEADS = 16
FF = 3072
CHAN = 4
PATCH = 2
LAT = 64
IMAGES = 4


def draw_timesteps(key, part):
    first, second, third, fourth, fifth = jax.random.split(key, 5)
    total = jax.random.randint(first, (IMAGES,), 0, 1000) + jax.random.randint(second, (IMAGES,), 0, 1000) + jax.random.randint(third, (IMAGES,), 0, 1000)
    base = (total // 3).astype(jnp.int32)
    top_index = jax.random.randint(fourth, (), 0, IMAGES)
    low_index = (top_index + 1 + jax.random.randint(fifth, (), 0, IMAGES - 1)) % IMAGES
    places = jnp.arange(IMAGES, dtype=jnp.int32)
    base = jnp.where(places == top_index, 999, base)
    base = jnp.where(places == low_index, 0, base)
    return base.astype(jnp.int32)


def shard_levels(own_key, extent, pieces, low, high):
    def one(dim, blocks):
        draws = jax.random.uniform(jax.random.fold_in(jax.random.fold_in(own_key, 6), dim), (blocks,), jnp.float32, low / len(pieces), high / len(pieces))
        return jnp.repeat(jnp.exp(draws), extent[dim] // blocks).reshape((-1,) + (1,) * (len(extent) - dim - 1))

    gain = one(*pieces[0])
    for cut in pieces[1:]:
        gain = gain * one(*cut)
    return gain


def gaussian(rng, dims, deviation, most, shards=(), held_as=jnp.bfloat16):
    gain = shard_levels(rng, dims, shards, -0.22, 0.18) if shards else 1.0
    entries = jax.random.normal(rng, dims, jnp.float32) * deviation * gain
    return jnp.minimum(jnp.maximum(entries, -most), most).astype(held_as)


def setup_inputs(seed: int = 0) -> dict:
    streams_of = jax.random.split(jax.random.key(seed), 18)
    return {
        "latent": gaussian(streams_of[0], (IMAGES, LAT, LAT, CHAN), 1.0, 6.0, ((0, 2), (1, 4), (2, 4)), jnp.float32),
        "noise": gaussian(streams_of[1], (IMAGES, LAT, LAT, CHAN), 1.0, 6.0, ((0, 2), (1, 4), (2, 4)), jnp.float32),
        "timesteps": draw_timesteps(jax.random.fold_in(streams_of[17], 71), 0),
        "condition": gaussian(streams_of[3], (IMAGES, LAT // PATCH, LAT // PATCH, D), 1.0, 6.0, ((0, 2), (1, 4), (2, 4))),
        "embed_weight": gaussian(streams_of[4], (PATCH * PATCH * CHAN, D), (PATCH * PATCH * CHAN) ** -0.5, 1.5, (), jnp.float32),
        "embed_bias": gaussian(streams_of[5], (D,), 0.5, 3.0, (), jnp.float32),
        "modulation": gaussian(streams_of[6], (D, 6 * D), D ** -0.5, 0.1875, ((0, 16),)),
        "modulation_bias": gaussian(streams_of[7], (6 * D,), 0.3, 2.0, (), jnp.float32),
        "project_in": gaussian(streams_of[8], (D, 3 * D), D ** -0.5, 0.1875, ((0, 16),)),
        "project_out": gaussian(streams_of[9], (D, D), (D // 64) ** -0.5, 1.5, ((0, 16),)),
        "gate_up": gaussian(streams_of[10], (D, 2 * FF), D ** -0.5, 0.1875, ((0, 16),)),
        "down_weight": gaussian(streams_of[11], (FF, D), FF ** -0.5, 0.109375, ((0, 16),)),
        "final_modulation": gaussian(streams_of[12], (D, 2 * D), D ** -0.5, 0.1875, ((0, 16),)),
        "final_offsets": gaussian(streams_of[13], (2 * D,), 0.3, 2.0, (), jnp.float32),
        "final_weight": gaussian(streams_of[14], (D, PATCH * PATCH * CHAN), D ** -0.5, 0.1875, (), jnp.float32),
        "final_bias": gaussian(streams_of[15], (PATCH * PATCH * CHAN,), 0.3, 2.0, (), jnp.float32),
        "cotangent": gaussian(streams_of[16], (IMAGES, LAT, LAT, CHAN), 1.0, 6.0, ((0, 2), (1, 4), (2, 4)), jnp.float32),
    }


@jax.custom_vjp
def low(v):
    return lax.optimization_barrier(v.astype(jnp.bfloat16)).astype(jnp.float32)

@jax.custom_vjp
def low_back(v):
    return v

def low_keep(v):
    return (low(v), None)

def low_pass(kept, grad):
    return (grad,)

def back_keep(v):
    return (v, None)

def back_low(kept, grad):
    return (low(grad),)
low.defvjp(low_keep, low_pass)
low_back.defvjp(back_keep, back_low)
EPSILON = 1e-06

def product(left, right):
    return jnp.dot(left, right, precision=lax.Precision.HIGHEST, preferred_element_type=jnp.float32)

def modnorm(rows, scale, shift):
    normed = rows * lax.rsqrt(lax.optimization_barrier(jnp.mean(rows * rows, axis=-1, keepdims=True)) + EPSILON)
    return normed * (1.0 + scale) + shift

def unfold(tile):
    count, height, across, chans = tile.shape
    cut = tile.reshape(count, height // PATCH, PATCH, across // PATCH, PATCH, chans)
    return cut.transpose(0, 1, 3, 2, 4, 5).reshape(count * (height // PATCH) * (across // PATCH), PATCH * PATCH * chans)

def refold(flat, count, height, across, chans):
    cut = flat.reshape(count, height // PATCH, across // PATCH, PATCH, PATCH, chans)
    return cut.transpose(0, 1, 3, 2, 4, 5).reshape(count, height, across, chans)

def forward(clean, noise_img, time, cond, embed_weight, embed_bias, modulation, modulation_bias, project_in, project_out, gate_up, down_weight, final_modulation, final_offsets, final_weight, final_bias):
    highest = lax.Precision.HIGHEST
    noisy = (1.0 - time) * clean + time * noise_img
    aligned = jnp.roll(noisy, (1, 1), axis=(0, 1))[None]
    patches = unfold(aligned)
    embedded = product(patches, embed_weight) + embed_bias
    cond_act = low(jax.nn.silu(cond.reshape(-1, D)))
    mod_rows = low_back(product(cond_act, modulation)) + modulation_bias
    shift_a, scale_a, gate_a, shift_b, scale_b, gate_b = jnp.split(mod_rows, 6, axis=1)
    final_rows = low_back(product(cond_act, final_modulation)) + final_offsets
    shift_f, scale_f = jnp.split(final_rows, 2, axis=1)
    attend_in = low(modnorm(embedded, scale_a, shift_a))
    qkv = low(low_back(product(attend_in, project_in)))
    head = D // HEADS
    queries = qkv[:, :D].reshape(-1, HEADS, head)
    keys = qkv[:, D:2 * D].reshape(-1, HEADS, head)
    values = qkv[:, 2 * D:].reshape(-1, HEADS, head)
    scores = low_back(jnp.einsum('qhd,khd->hqk', queries, keys, precision=highest) * (1.0 / math.sqrt(head)))
    probs = low(jax.nn.softmax(scores, axis=-1))
    mixed = low(low_back(jnp.einsum('hqk,khd->qhd', probs, values, precision=highest))).reshape(-1, D)
    branch = low_back(product(mixed, project_out))
    h_one = embedded + gate_a * branch
    ffn_in = low(modnorm(h_one, scale_b, shift_b))
    gateup = low_back(product(ffn_in, gate_up))
    hidden = low(jax.nn.silu(gateup[:, :FF]) * gateup[:, FF:])
    ffn = low_back(product(hidden, down_weight))
    h_two = h_one + gate_b * ffn
    final_in = modnorm(h_two, scale_f, shift_f)
    rows_out = product(final_in, final_weight) + final_bias
    tile = refold(rows_out, 1, LAT, LAT, CHAN)[0]
    return jnp.roll(tile, (-1, -1), axis=(0, 1))

def reference(latent, noise, timesteps, condition, embed_weight, embed_bias, modulation, modulation_bias, project_in, project_out, gate_up, down_weight, final_modulation, final_offsets, final_weight, final_bias, cotangent):
    times = timesteps.astype(jnp.float32) / 1000.0
    params = (embed_weight, embed_bias, modulation.astype(jnp.float32), modulation_bias, project_in.astype(jnp.float32), project_out.astype(jnp.float32), gate_up.astype(jnp.float32), down_weight.astype(jnp.float32), final_modulation.astype(jnp.float32), final_offsets, final_weight, final_bias)
    cond_all = condition.astype(jnp.float32)

    def one_image(totals, items):
        clean, noise_img, time, cond_img, pulled = items

        def run(clean_in, cond_in, *weights):
            return forward(clean_in, noise_img, time, cond_in, *weights)
        pred, pull = jax.vjp(run, clean, cond_img, *params)
        grads = pull(pulled)
        totals = tuple((a + b for a, b in zip(totals, grads[2:])))
        return (totals, (pred, grads[0], grads[1]))
    start = tuple((jnp.zeros_like(p) for p in params))
    totals, (prediction, latent_grad, condition_grad) = lax.scan(one_image, start, (latent, noise, times, cond_all, cotangent))
    return (prediction, latent_grad, condition_grad, totals[0], totals[1], totals[2], totals[3], totals[4], totals[5], totals[6], totals[7], totals[8], totals[9], totals[10], totals[11])
```

```python
import functools
import math

import jax
import jax.numpy as jnp
from jax import lax
from jax.experimental import pallas as pl
from jax.experimental.pallas import tpu as pltpu
from jax.sharding import Mesh
from jax.sharding import PartitionSpec as P

HEADS = 16
PATCH = 2
EPSILON = 1e-06
MESH = pl.DeviceIdType.MESH
BF16 = jnp.bfloat16
F32 = jnp.float32
RANKS = 8


def rank_of():
    return lax.axis_index("l") * 4 + lax.axis_index("gx")


def in_group(rank):
    return {"l": rank // 4, "gx": lax.rem(rank, 4)}


def in_plane(place):
    return {"h": place // 8, "l": lax.rem(place // 4, 2), "gx": lax.rem(place, 4)}


CHIPS = 4


class Place:
    def __init__(self):
        self.l = lax.axis_index("l")
        across = lax.axis_index("gx")
        self.y = lax.div(across, 2)
        self.core = lax.rem(across, 2)

    def chip(self, k):
        dl, dy = lax.div(k, 2), lax.rem(k, 2)
        return self.l + dl - 2 * self.l * dl, self.y + dy - 2 * self.y * dy

    def rows(self, k):
        row, col = self.chip(k)
        return pl.ds((row * 2 + col) * 2, 2)

    def slot(self, k, flip):
        row, col = self.chip(k)
        return (row * 2 + col) * 2 + (1 - self.core if flip else self.core)

    def device(self, k, flip):
        row, col = self.chip(k)
        return {"l": row, "gx": col * 2 + (1 - self.core if flip else self.core)}

    def greet(self, everyone, across=False):
        barrier = pltpu.get_barrier_semaphore()
        peers = [(0, True)] + [(k, False) for k in range(1, CHIPS)]
        if everyone:
            peers += [(k, True) for k in range(1, CHIPS)]
        for k, flip in peers:
            pl.semaphore_signal(barrier, inc=1, device_id=self.device(k, flip), device_id_type=MESH)
        if across:
            other = {"x": 1 - lax.axis_index("x")}
            pl.semaphore_signal(barrier, inc=1, device_id=other, device_id_type=MESH)
        pl.semaphore_wait(barrier, len(peers) + across)


def sent(src, dst, sems, kind, k, device):
    return pltpu.make_async_remote_copy(
        src_ref=src, dst_ref=dst, send_sem=sems.at[kind, k], recv_sem=sems.at[kind + 1, k],
        device_id=device, device_id_type=MESH,
    )


class Gather:
    def __init__(self, place, buf, sems):
        self.place, self.buf, self.sems = place, buf, sems

    def link(self, k):
        mine = self.buf.at[self.place.slot(0, False)]
        return sent(mine, mine, self.sems, 0, k, self.place.device(k, False))

    def pair(self, k):
        block = self.buf.at[self.place.slot(k, False)]
        return sent(block, block, self.sems, 2, k, self.place.device(0, True))

    def start(self):
        for k in range(1, CHIPS):
            self.link(k).start()
        self.pair(0).start()

    def arrive(self, k):
        def forward(n):
            self.link(n).wait_recv()
            self.pair(n).start()

        @pl.when(k == 1)
        def _():
            forward(1)
            forward(2)

        @pl.when(k == 3)
        def _():
            forward(3)

        self.pair(k).wait_recv()

    def finish(self):
        for k in range(CHIPS):
            if k:
                self.link(k).wait_send()
            self.pair(k).wait_send()


class Scatter:
    def __init__(self, place, refs, sems):
        self.place, self.sems = place, sems
        self.both, self.got, self.out, self.land, self.total = refs

    def pair(self, k):
        return sent(
            self.both.at[k, 1 - self.place.core], self.got.at[k], self.sems, 4, k,
            self.place.device(0, True),
        )

    def link(self, k):
        return sent(self.out.at[k], self.land.at[k], self.sems, 6, k, self.place.device(k, False))

    def put(self, k, part):
        self.both[k] = part.astype(BF16).reshape(self.both.shape[1:])
        self.pair(k).start()

    def pass_on(self, k):
        self.pair(k).wait_recv()
        added = self.both[k, self.place.core].astype(F32) + self.got[k].astype(F32)

        @pl.when(k == 0)
        def _():
            self.total[...] = added

        @pl.when(k > 0)
        def _():
            self.out[k] = added.astype(BF16)
            self.link(k).start()

    def finish(self):
        for k in range(1, CHIPS):
            self.link(k).wait_recv()
            self.total[...] += self.land[k].astype(F32)
        for k in range(CHIPS):
            if k:
                self.link(k).wait_send()
            self.pair(k).wait_send()


def scatter_scratch(rows, width):
    return [
        pltpu.VMEM((CHIPS, 2, rows, width), BF16),
        pltpu.VMEM((CHIPS, rows, width), BF16),
        pltpu.VMEM((CHIPS, rows, width), BF16),
        pltpu.VMEM((CHIPS, rows, width), BF16),
    ]


def chips(body):
    lax.fori_loop(0, CHIPS, lambda k, carry: (body(k), carry)[1], 0)


def mat(value):
    return value.reshape(-1, value.shape[-1])


def product(left, right, contract):
    return lax.dot_general(
        left, right, ((contract[:1], contract[1:]), ((), ())), preferred_element_type=F32
    )


def grads_into(out_ref, left_ref, right_ref, pick=None, tile=128):
    right = mat(right_ref[...])

    def body(i, carry):
        cols = pl.ds(pl.multiple_of(i * tile, tile), tile)
        part = product(mat(left_ref[:, :, cols]), right, (0, 0)).astype(out_ref.dtype)
        if pick is not None:
            part = product(part, pick, (1, 0)).astype(out_ref.dtype)
        out_ref[cols, :] = part
        return carry

    lax.fori_loop(0, left_ref.shape[-1] // tile, body, 0)


def attend_kernel(
    factor, head, own, in_narrow, out_weight, total, attend_all, qkv, mixed, in_weight,
    both, got, out, land, sems,
):
    place = Place()
    place.greet(False)
    attend_all[place.slot(0, False)] = own[...]
    gather = Gather(place, attend_all, sems)
    gather.start()
    lanes = mixed.shape[-1] // 2
    pick = selection(6 * lanes, head, lanes)
    in_weight[...] = product(in_narrow[...], pick, (1, 1)).astype(BF16)

    def first(k):
        gather.arrive(k)
        rows = place.rows(k)
        part = product(mat(attend_all[rows]), in_weight[...], (1, 0)).astype(BF16)
        qkv[rows] = part.reshape(2, -1, part.shape[-1])

    chips(first)
    gather.finish()
    scatter = Scatter(place, (both, got, out, land, total), sems)

    def second(step):
        k = CHIPS - 1 - step
        rows = place.rows(k)
        for head in range(2):
            span = [pl.ds((part * 2 + head) * lanes, lanes) for part in range(3)]
            queries = mat(qkv[rows, :, span[0]])
            keys, values = mat(qkv[:, :, span[1]]), mat(qkv[:, :, span[2]])
            scores = product(keys, queries, (1, 1)) * factor
            expo = jnp.exp(scores - jnp.max(scores, axis=0, keepdims=True))
            probs = expo * (1.0 / jnp.sum(expo, axis=0, keepdims=True))
            gained = product(probs.astype(BF16), values, (0, 0)).astype(BF16)
            mixed[rows, :, span[0]] = gained.reshape(2, -1, lanes)
        scatter.put(k, product(mat(mixed[rows]), out_weight[...], (1, 0)))

        @pl.when(step > 0)
        def _():
            scatter.pass_on(k + 1)

    chips(second)
    scatter.pass_on(0)
    scatter.finish()


def feed_kernel(own, gate_weight, down_weight, total, ffn_all, gateup, both, got, out, land, sems):
    place = Place()
    place.greet(False)
    ffn_all[place.slot(0, False)] = own[...]
    gather = Gather(place, ffn_all, sems)
    gather.start()
    scatter = Scatter(place, (both, got, out, land, total), sems)
    share = down_weight.shape[0]

    def body(k):
        gather.arrive(k)
        rows = place.rows(k)
        part = product(mat(ffn_all[rows]), gate_weight[...], (1, 0))
        gateup[rows] = part.reshape(2, -1, 2 * share)
        gate, up = part[:, :share], part[:, share:]
        hidden = (gate * sigma(gate) * up).astype(BF16)
        scatter.put(k, product(hidden, down_weight[...], (1, 0)))

        @pl.when(k > 0)
        def _():
            scatter.pass_on(k - 1)

    chips(body)
    scatter.pass_on(CHIPS - 1)
    gather.finish()
    scatter.finish()


def feed_back_kernel(
    own, gate_weight, down_weight, gateup, ffn_all, total, gate_grad, down_grad,
    grad_all, grad_gateup, hidden_all, both, got, out, land, sems,
):
    place = Place()
    place.greet(False)
    grad_all[place.slot(0, False)] = own[...]
    gather = Gather(place, grad_all, sems)
    gather.start()
    scatter = Scatter(place, (both, got, out, land, total), sems)
    share = down_weight.shape[0]

    def body(k):
        gather.arrive(k)
        rows = place.rows(k)
        grad_hidden = product(mat(grad_all[rows]), down_weight[...], (1, 1))
        part = mat(gateup[rows])
        gate, up = part[:, :share], part[:, share:]
        gate_sigma = sigma(gate)
        silu = gate * gate_sigma
        hidden_all[rows] = (silu * up).astype(BF16).reshape(2, -1, share)
        grad_gate = grad_hidden * up * gate_sigma * (1.0 + gate * (1.0 - gate_sigma))
        both_grads = jnp.concatenate([grad_gate, grad_hidden * silu], 1).astype(BF16)
        grad_gateup[rows] = both_grads.reshape(2, -1, 2 * share)
        scatter.put(k, product(both_grads, gate_weight[...], (1, 1)))

        @pl.when(k > 0)
        def _():
            scatter.pass_on(k - 1)

    chips(body)
    scatter.pass_on(CHIPS - 1)
    gather.finish()
    grads_into(down_grad, hidden_all, grad_all)
    grads_into(gate_grad, ffn_all, grad_gateup)
    scatter.finish()


def attend_back_kernel(
    factor, head_size, own, in_weight, out_weight, attend_all, qkv, mixed, gate_grad, down_grad,
    total, in_grad, out_grad, gate_land, down_land,
    grad_all, grad_mixed, grad_qkv, key_sum, value_sum, both, got, out, land, cross, sems,
):
    place = Place()
    place.greet(False, True)
    crossings = (
        Crossing(gate_grad, gate_land, cross, 0, gate_land.shape[1]),
        Crossing(down_grad, down_land, cross, 1, down_land.shape[0], False),
    )
    for crossing in crossings:
        crossing.start()
    grad_all[place.slot(0, False)] = own[...]
    gather = Gather(place, grad_all, sems)
    gather.start()
    lanes = mixed.shape[-1] // 2
    key_sum[...] = jnp.zeros_like(key_sum)
    value_sum[...] = jnp.zeros_like(value_sum)

    def first(k):
        gather.arrive(k)
        rows = place.rows(k)
        part = product(mat(grad_all[rows]), out_weight[...], (1, 1)).astype(BF16)
        grad_mixed[rows] = part.reshape(2, -1, 2 * lanes)
        for head in range(2):
            span = [pl.ds((part * 2 + head) * lanes, lanes) for part in range(3)]
            queries, grads = mat(qkv[rows, :, span[0]]), mat(grad_mixed[rows, :, span[0]])
            keys, values = mat(qkv[:, :, span[1]]), mat(qkv[:, :, span[2]])
            scores = product(keys, queries, (1, 1)) * factor
            expo = jnp.exp(scores - jnp.max(scores, axis=0, keepdims=True))
            probs = expo * (1.0 / jnp.sum(expo, axis=0, keepdims=True))
            value_sum[head] += product(probs.astype(BF16), grads, (1, 0))
            grad_probs = product(values, grads, (1, 1))
            middle = jnp.sum(grad_probs * probs, axis=0, keepdims=True)
            grad_scores = (probs * (grad_probs - middle)).astype(BF16)
            key_sum[head] += product(grad_scores, queries, (1, 0))
            back = (product(grad_scores, keys, (0, 0)) * factor).astype(BF16)
            grad_qkv[rows, :, span[0]] = back.reshape(2, -1, lanes)

    chips(first)
    gather.finish()
    for head in range(2):
        span = [pl.ds((part * 2 + head) * lanes, lanes) for part in range(3)]
        high = grad_qkv.shape[1]
        keys = (key_sum[head] * factor).astype(BF16)
        grad_qkv[:, :, span[1]] = keys.reshape(-1, high, lanes)
        grad_qkv[:, :, span[2]] = value_sum[head].astype(BF16).reshape(-1, high, lanes)
    scatter = Scatter(place, (both, got, out, land, total), sems)

    def second(step):
        k = CHIPS - 1 - step
        scatter.put(k, product(mat(grad_qkv[place.rows(k)]), in_weight[...], (1, 1)))

        @pl.when(step > 0)
        def _():
            scatter.pass_on(k + 1)

    chips(second)
    scatter.pass_on(0)
    grads_into(out_grad, mixed, grad_all)
    pick = selection(6 * lanes, head_size, lanes)
    grads_into(in_grad, attend_all, grad_qkv, pick)
    scatter.finish()
    for crossing in crossings:
        crossing.wait()


def mod_back_kernel(
    own, weight, cond_all, in_grad, out_grad, total, mod_grad, in_land, out_land,
    grad_all, both, got, out, land, cross, sems,
):
    place = Place()
    place.greet(True, True)
    crossings = (
        Crossing(in_grad, in_land, cross, 0, in_land.shape[1]),
        Crossing(out_grad, out_land, cross, 1, out_land.shape[0], False),
    )
    for crossing in crossings:
        crossing.start()
    me = place.slot(0, False)

    def give(k, flip):
        return sent(
            own.at[place.slot(k, flip)], grad_all.at[me], sems, 2 if flip else 0, k,
            place.device(k, flip),
        )

    for k in range(1, CHIPS):
        for flip in (False, True):
            give(k, flip).start()
    give(0, True).start()
    grad_all[me] = own[me]
    scatter = Scatter(place, (both, got, out, land, total), sems)

    def body(k):
        give(k, True).wait_recv()

        @pl.when(k > 0)
        def _():
            give(k, False).wait_recv()

        scatter.put(k, product(mat(grad_all[place.rows(k)]), weight[...], (1, 1)))

        @pl.when(k > 0)
        def _():
            scatter.pass_on(k - 1)

    chips(body)
    scatter.pass_on(CHIPS - 1)
    grads_into(mod_grad, cond_all, grad_all)
    for k in range(CHIPS):
        give(k, True).wait_send()
        if k:
            give(k, False).wait_send()
    scatter.finish()
    for crossing in crossings:
        crossing.wait()


def segment(kernel, number, operands, outs, scratch, scatters, crosses=False):
    work = [pltpu.VMEM(shape, kind) for shape, kind in scratch]
    work += scatter_scratch(*scatters)
    if crosses:
        work.append(pltpu.SemaphoreType.DMA((2, 2, RANKS)))
    name = getattr(kernel, "func", kernel).__name__
    return pl.pallas_call(
        kernel,
        out_shape=tuple(jax.ShapeDtypeStruct(shape, kind) for shape, kind in outs),
        in_specs=[pl.BlockSpec(memory_space=pltpu.VMEM)] * len(operands),
        out_specs=tuple(pl.BlockSpec(memory_space=pltpu.VMEM) for _ in outs),
        scratch_shapes=[*work, pltpu.SemaphoreType.DMA((8, CHIPS))],
        compiler_params=pltpu.CompilerParams(
            collective_id=number, has_side_effects=True, vmem_limit_bytes=60 << 20
        ),
        name=name,
    )(*operands)


PLACES = 2 * RANKS


def copied(src, dst, send_sem, recv_sem, device):
    return pltpu.make_async_remote_copy(
        src_ref=src, dst_ref=dst, send_sem=send_sem, recv_sem=recv_sem,
        device_id=device, device_id_type=MESH,
    )


def greet_plane(me, half):
    barrier = pltpu.get_barrier_semaphore()
    for step in range(1, PLACES):
        pl.semaphore_signal(
            barrier, inc=1, device_id=in_plane(lax.rem(me + step, PLACES)), device_id_type=MESH
        )
    pl.semaphore_signal(barrier, inc=1, device_id={"x": 1 - half}, device_id_type=MESH)
    pl.semaphore_wait(barrier, PLACES)


def loop(count, body):
    lax.fori_loop(0, count, lambda i, carry: (body(i), carry)[1], 0)


def start_kernel(
    modulation, final_modulation, gate_up, in_cols, project_out, down, condition,
    mods, cond_all, cond_own, mod_w, gate_w, in_w, out_w, down_w,
    stage, sems, w_send, w_recv, xs_send, xs_recv, r_send, r_recv, own_sem, c_sem,
):
    place = Place()
    half, group, rank = lax.axis_index("x"), lax.axis_index("h"), rank_of()
    me = group * RANKS + rank
    high, width = project_out.shape
    share = gate_w.shape[1] // 2
    blocks = modulation.shape[1] // width
    across = {"x": 1 - half}
    mine = lax.div(me, 2)
    sends = lax.rem(me, 2) == half
    pad = out_w.shape[1] - high
    out_w[:, pl.ds(high, pad)] = jnp.zeros((2, pad, width), BF16)
    greet_plane(me, half)

    partner = copied(
        condition.at[1 - group], cond_own.at[group], c_sem.at[0], c_sem.at[1], {"h": 1 - group}
    )
    partner.start()

    def rows_of(number):
        return pl.ds(pl.multiple_of(number * high, 8), high)

    def lanes_of(number, count):
        return pl.ds(pl.multiple_of(number * count, 128), count)

    def source_of(kind, target, then):
        if kind == 0:

            @pl.when(target < blocks)
            def _():
                then(modulation.at[:, lanes_of(target, width)])

            @pl.when(target >= blocks)
            def _():
                then(final_modulation.at[:, lanes_of(target - blocks, width)])
        elif kind == 3:
            then(in_cols.at[target])
        else:
            then(gate_up.at[:, lanes_of((kind - 1) * RANKS + target, share)])

    def landing(kind, number):
        if kind == 0:
            return mod_w.at[rows_of(number)]
        if kind == 3:
            return in_w.at[rows_of(number)]
        return gate_w.at[rows_of(number), pl.ds((kind - 1) * share, share)]

    def cast(kinds):
        @pl.when(sends)
        def _():
            for kind in kinds:
                source_of(
                    kind, rank,
                    lambda src: pltpu.make_async_copy(
                        src, landing(kind, me), own_sem.at[kind]
                    ).start(),
                )

            def body(i):
                target = lax.rem(me + 1 + i, PLACES)
                for kind in kinds:
                    source_of(
                        kind, lax.rem(target, RANKS),
                        lambda src: copied(
                            src, landing(kind, me), w_send.at[kind, i], w_recv.at[kind, mine],
                            in_plane(target),
                        ).start(),
                    )

            loop(PLACES - 1, body)

    def swap(kind, number):
        block = (mod_w, gate_w, in_w)[kind].at[rows_of(2 * number + half)]
        return copied(block, block, xs_send.at[kind, number], xs_recv.at[kind, number], across)

    def take(kinds, swap_kinds):
        def body(i):
            number = lax.rem(lax.div(me + PLACES - half, 2) + RANKS - i, RANKS)
            source = 2 * number + half

            @pl.when(source != me)
            def _():
                for kind in kinds:
                    block = landing(kind, source)
                    copied(
                        block, block, w_send.at[kind, 0], w_recv.at[kind, number], across
                    ).wait_recv()

            @pl.when(source == me)
            def _():
                for kind in kinds:
                    block = landing(kind, me)
                    pltpu.make_async_copy(block, block, own_sem.at[kind]).wait()

            for kind in swap_kinds:
                swap(kind, number).start()

        loop(RANKS, body)

    def row_copy(which, target_group):
        src, dst = ((project_out, out_w.at[half, pl.ds(0, high)]), (down, down_w.at[half]))[which]
        return copied(
            src, dst, r_send.at[which, target_group], r_recv.at[which, 0],
            in_plane(target_group * RANKS + mine),
        )

    def row_own(which):
        src, dst = ((project_out, out_w.at[half, pl.ds(0, high)]), (down, down_w.at[half]))[which]
        return pltpu.make_async_copy(src, dst, own_sem.at[4 + which])

    def row_swap(which):
        block = (out_w.at[half, pl.ds(0, high)], down_w.at[half])[which]
        return copied(block, block, r_send.at[which, 2], r_recv.at[which, 1], across)

    cast((0,))
    cond_own[group] = condition[group]
    partner.wait()
    raw = cond_own[...].astype(F32)
    cond_all[rank] = mat(raw * sigma(raw)).astype(BF16)
    gather = Gather(place, cond_all, sems)
    gather.start()
    cast((3, 1, 2))
    for which in range(2):
        for target_group in range(2):
            target = target_group * RANKS + mine

            @pl.when(sends & (target != me))
            def _():
                row_copy(which, target_group).start()

            @pl.when(sends & (target == me))
            def _():
                row_own(which).start()

    take((0,), (0,))

    def across_in(kind):
        def body(number):
            swap(kind, number).wait_recv()

        loop(RANKS, body)

    across_in(0)

    def give(k, flip):
        core = 1 - place.core if flip else place.core
        return sent(
            stage.at[k, core], mods.at[rank], sems, 6 if flip else 4, k, place.device(k, flip)
        )

    def body(k):
        gather.arrive(k)
        part = product(mat(cond_all[place.rows(k)]), mod_w[...], (1, 0)).astype(BF16)
        stage[k] = part.reshape(stage.shape[1:])
        give(k, True).start()

        @pl.when(k == 0)
        def _():
            mods[rank] = stage[0, place.core]

        @pl.when(k > 0)
        def _():
            give(k, False).start()

    chips(body)
    take((3, 1, 2), (2, 1))
    owner = 2 * rank + half
    for which in range(2):

        @pl.when(owner != me)
        def _():
            row_copy(which, 0).wait_recv()

        @pl.when(owner == me)
        def _():
            row_own(which).wait()

        row_swap(which).start()
    gather.finish()
    for k in range(CHIPS):
        give(k, True).wait()
        if k:
            give(k, False).wait()
    across_in(1)
    across_in(2)
    for which in range(2):
        row_swap(which).wait()
        for target_group in range(2):

            @pl.when(sends & (target_group * RANKS + mine != me))
            def _():
                row_copy(which, target_group).wait_send()

    @pl.when(sends)
    def _():
        def drain(i):
            for kind in range(4):
                block = landing(kind, me)
                copied(block, block, w_send.at[kind, i], w_recv.at[kind, 0], across).wait_send()

        loop(PLACES - 1, drain)

    def swapped_out(number):
        for kind in range(3):
            swap(kind, number).wait_send()

    loop(RANKS, swapped_out)


def start(modulation, final_modulation, gate_up, in_cols, project_out, down, condition):
    high, width = project_out.shape
    share = gate_up.shape[1] // (2 * RANKS)
    tokens = condition.shape[0] * condition.shape[1]
    outs = [
        (RANKS, tokens, width), (RANKS, tokens, width), condition.shape, (width, width),
        (width, 2 * share), (width, in_cols.shape[2]), (2, 128, width), (2, *down.shape),
    ]
    dma = pltpu.SemaphoreType.DMA
    return pl.pallas_call(
        start_kernel,
        out_shape=tuple(jax.ShapeDtypeStruct(shape, BF16) for shape in outs),
        in_specs=[pl.BlockSpec(memory_space=pl.ANY)] * 6 + [pl.BlockSpec(memory_space=pltpu.VMEM)],
        out_specs=tuple(pl.BlockSpec(memory_space=pltpu.VMEM) for _ in outs),
        scratch_shapes=[
            pltpu.VMEM((CHIPS, 2, tokens, width), BF16),
            dma((8, CHIPS)),
            dma((4, PLACES)), dma((4, RANKS)), dma((3, RANKS)), dma((3, RANKS)),
            dma((2, 3)), dma((2, 2)), dma((6,)), dma((2,)),
        ],
        compiler_params=pltpu.CompilerParams(
            collective_id=2, has_side_effects=True, vmem_limit_bytes=60 << 20
        ),
        name="start_kernel",
    )(modulation, final_modulation, gate_up, in_cols, project_out, down, condition)


class Crossing:
    def __init__(self, grads, land, sems, kind, high, by_place=True):
        self.grads, self.land, self.sems, self.kind = grads, land, sems, kind
        self.half, self.high, self.by_place = lax.axis_index("x"), high, by_place

    def copy(self, number, order):
        if self.by_place:
            first = (2 * number + 1 - self.half) * self.high
            block, land = self.grads.at[pl.ds(pl.multiple_of(first, 8), self.high)], self.land.at[number]
        else:
            first = (1 - self.half) * (self.grads.shape[0] // 2)
            block, land = self.grads.at[pl.ds(pl.multiple_of(first, 8), self.high)], self.land
        return copied(
            block, land, self.sems.at[self.kind, 0, order], self.sems.at[self.kind, 1, order],
            {"x": 1 - self.half},
        )

    def start(self):
        if self.by_place:
            loop(RANKS, lambda i: self.copy(i, i).start())
        else:
            self.copy(0, 0).start()

    def wait(self):
        if self.by_place:
            loop(RANKS, lambda i: self.copy(i, i).wait())
        else:
            self.copy(0, 0).wait()


def finish_kernel(
    mod_grad, gate_grad, gate_land, in_grad, in_land, down_grad, down_land, out_grad, out_land, small,
    mod_out, gate_out, in_out, down_out, out_out, small_out,
    mod_land, mod_stage, gate_stage, in_stage, down_stage, out_stage,
    mod_in, gate_in, in_in, down_in, out_in, small_in, small_sum, small_land,
    cross, send, recv, r_send, r_recv, x_send, x_recv, s_send, s_recv, sx_sem,
):
    half, group, rank = lax.axis_index("x"), lax.axis_index("h"), rank_of()
    me = group * RANKS + rank
    mine = lax.div(me, 2)
    high = mod_land.shape[1]
    across = {"x": 1 - half}
    owns = lax.rem(me, 2) == half
    greet_plane(me, half)
    mods = Crossing(mod_grad, mod_land, cross, 0, high)
    loop(RANKS, lambda i: mods.copy(lax.rem(mine + i, RANKS), i).start())

    def small_copy(step):
        other = lax.rem(me + step, PLACES)
        return copied(
            small.at[other], small_in.at[me], s_send.at[0, step], s_recv.at[0, step], in_plane(other)
        )

    loop(PLACES - 1, lambda i: small_copy(i + 1).start())
    small_in[me] = small[me]

    def own_rows(ref, number):
        first = pl.multiple_of((2 * number + half) * high, 8)
        return ref[pl.ds(first, high)].astype(F32)

    def pieces(kind):
        return ((mod_stage, mod_in), (gate_stage, gate_in), (in_stage, in_in))[kind]

    def scatter(kind, number):
        stage, landing = pieces(kind)
        return copied(
            stage.at[number], landing.at[me], send.at[kind, number], recv.at[kind, me],
            in_plane(2 * number + half),
        )

    def push(kind, grads, land, number):
        stage, landing = pieces(kind)
        stage[number] = (own_rows(grads, number) + land[number].astype(F32)).astype(BF16)

        @pl.when(2 * number + half != me)
        def _():
            scatter(kind, number).start()

        @pl.when(2 * number + half == me)
        def _():
            landing[me] = stage[number]

    def early(i):
        number = lax.rem(mine + i, RANKS)
        push(1, gate_grad, gate_land, number)
        push(2, in_grad, in_land, number)

    loop(RANKS, early)
    owner = 2 * rank + half
    rows = (
        (down_stage, down_in, down_grad, down_land, down_out),
        (out_stage, out_in, out_grad, out_land, out_out),
    )

    def row_copy(which, source_group):
        stage, landing = rows[which][:2]
        return copied(
            stage, landing.at[group], r_send.at[which], r_recv.at[which, source_group], in_plane(owner)
        )

    for which, (stage, landing, grads, land, _) in enumerate(rows):
        first = pl.multiple_of(half * (grads.shape[0] // 2), 8)
        kept = grads[pl.ds(first, land.shape[0])].astype(F32)
        stage[...] = (kept + land[...].astype(F32)).astype(BF16)
        for source_group in range(2):

            @pl.when((owner != me) & (group == source_group))
            def _():
                row_copy(which, source_group).start()

        @pl.when(owner == me)
        def _():
            landing[group] = stage[...]

    def late(i):
        number = lax.rem(mine + i, RANKS)
        mods.copy(number, i).wait()
        push(0, mod_grad, mod_land, number)

    loop(RANKS, late)

    loop(PLACES - 1, lambda i: small_copy(i + 1).wait())
    small_sum[...] = jnp.sum(small_in[...], axis=0)
    pair = copied(small_sum, small_land, sx_sem.at[0], sx_sem.at[1], across)
    pair.start()
    pair.wait()
    small_out[me] = small_sum[...] + small_land[...]

    def spread(step):
        other = lax.rem(me + step, PLACES)
        return copied(
            small_out.at[me], small_out.at[me], s_send.at[1, step], s_recv.at[1, step], in_plane(other)
        )

    loop(PLACES - 1, lambda i: spread(i + 1).start())

    def final(kind, index):
        if kind == 2:
            block = in_out
        else:
            out, count = (mod_out, gate_out)[kind], (mod_stage, gate_stage)[kind].shape[2]
            block = out.at[:, pl.ds(index * count, count)]
        return copied(block, block, x_send.at[kind, index], x_recv.at[kind, index], across)

    def final_rows(which):
        out = rows[which][4]
        return copied(out, out, x_send.at[3, which], x_recv.at[3, which], across)

    @pl.when(owns)
    def _():
        def got(kind, source):
            @pl.when(source != me)
            def _():
                landing = pieces(kind)[1].at[source]
                copied(
                    landing, landing, send.at[kind, 0], recv.at[kind, source], across
                ).wait_recv()

        for index in range(RANKS):
            got(1, index)
            got(1, RANKS + index)
            count = gate_stage.shape[2]
            added = gate_in[index].astype(F32) + gate_in[RANKS + index].astype(F32)
            gate_out[:, index * count : (index + 1) * count] = added.astype(BF16)
            final(1, index).start()
        for index in range(RANKS):
            got(2, index)
            got(2, RANKS + index)
            added = in_in[index].astype(F32) + in_in[RANKS + index].astype(F32)
            in_out[index] = added.astype(BF16)
        final(2, 0).start()
        for which, (_, landing, _, _, out) in enumerate(rows):
            for source_group in range(2):

                @pl.when(source_group * RANKS + mine != me)
                def _():
                    row_copy(which, source_group).wait_recv()

            out[...] = (landing[0].astype(F32) + landing[1].astype(F32)).astype(BF16)
            final_rows(which).start()
        for index in range(RANKS):
            got(0, index)
            got(0, RANKS + index)
            count = mod_stage.shape[2]
            added = mod_in[index].astype(F32) + mod_in[RANKS + index].astype(F32)
            mod_out[:, index * count : (index + 1) * count] = added.astype(BF16)
            final(0, index).start()
        for kind in range(2):
            for index in range(RANKS):
                final(kind, index).wait_send()
        final(2, 0).wait_send()
        for which in range(2):
            final_rows(which).wait_send()

    @pl.when(jnp.logical_not(owns))
    def _():
        for kind in range(2):
            for index in range(RANKS):
                final(kind, index).wait_recv()
        final(2, 0).wait_recv()
        for which in range(2):
            final_rows(which).wait_recv()

    loop(PLACES - 1, lambda i: spread(i + 1).wait())

    def drain(number):
        @pl.when(2 * number + half != me)
        def _():
            for kind in range(3):
                scatter(kind, number).wait_send()

    loop(RANKS, drain)
    for which in range(2):

        @pl.when(owner != me)
        def _():
            row_copy(which, 0).wait_send()


def finish(mod_grad, gate_grad, gate_land, in_grad, in_land, down_grad, down_land, out_grad, out_land, small):
    operands = (
        mod_grad, gate_grad, gate_land, in_grad, in_land, down_grad, down_land, out_grad, out_land, small,
    )
    high, width = out_land.shape
    gates, ins, downs = gate_grad.shape[1], in_grad.shape[1], down_land.shape[0]
    outs = [
        ((high, RANKS * width), BF16), ((high, RANKS * gates), BF16), ((RANKS, high, ins), BF16),
        ((downs, width), BF16), ((high, width), BF16), (small.shape, F32),
    ]
    work = [
        (RANKS, high, width), (RANKS, high, width), (RANKS, high, gates), (RANKS, high, ins),
        (downs, width), (high, width),
        (PLACES, high, width), (PLACES, high, gates), (PLACES, high, ins),
        (2, downs, width), (2, high, width),
    ]
    dma = pltpu.SemaphoreType.DMA
    return pl.pallas_call(
        finish_kernel,
        out_shape=tuple(jax.ShapeDtypeStruct(shape, kind) for shape, kind in outs),
        in_specs=[pl.BlockSpec(memory_space=pltpu.VMEM)] * len(operands),
        out_specs=tuple(pl.BlockSpec(memory_space=pltpu.VMEM) for _ in outs),
        scratch_shapes=[pltpu.VMEM(shape, BF16) for shape in work]
        + [pltpu.VMEM(small.shape, F32), pltpu.VMEM(small.shape[1:], F32), pltpu.VMEM(small.shape[1:], F32)]
        + [
            dma((1, 2, RANKS)), dma((3, RANKS)), dma((3, PLACES)), dma((2,)), dma((2, 2)),
            dma((4, RANKS)), dma((4, RANKS)), dma((2, PLACES)), dma((2, PLACES)), dma((2,)),
        ],
        compiler_params=pltpu.CompilerParams(
            collective_id=3, has_side_effects=True, vmem_limit_bytes=60 << 20
        ),
        name="finish_kernel",
    )(*operands)


def selection(wide_count, head, lanes):
    narrow = -(-(wide_count // lanes * head) // 128) * 128
    row = lax.broadcasted_iota(jnp.int32, (wide_count, narrow), 0)
    col = lax.broadcasted_iota(jnp.int32, (wide_count, narrow), 1)
    within = lax.rem(row, lanes)
    hit = (lax.div(row, lanes) * head + within == col) & (within < head)
    return jnp.where(hit, 1.0, 0.0).astype(BF16)


def shifted(shard, axes, by):
    size = math.prod(lax.axis_size(a) for a in axes)
    return lax.ppermute(shard, axes, [(i, (i + by) % size) for i in range(size)])


def swapped(both, group):
    kept = jnp.where(group == 0, both[0], both[1])
    sent = jnp.where(group == 0, both[1], both[0])
    got = lax.ppermute(sent, "h", [(0, 1), (1, 0)])
    return jnp.stack([jnp.where(group == 0, kept, got), jnp.where(group == 0, got, kept)])


def unfold(tile):
    count, height, across, chans = tile.shape
    cut = tile.reshape(count, height // PATCH, PATCH, across // PATCH, PATCH, chans)
    return cut.transpose(0, 1, 3, 2, 4, 5).reshape(count, -1, PATCH * PATCH * chans)


def refold(flat, count, height, across, chans):
    cut = flat.reshape(count, height // PATCH, across // PATCH, PATCH, PATCH, chans)
    return cut.transpose(0, 1, 3, 2, 4, 5).reshape(count, height, across, chans)


def normed(rows):
    inverse = lax.rsqrt(jnp.mean(rows * rows, axis=-1, keepdims=True) + EPSILON)
    return rows * inverse, inverse


def modnorm_back(grad, norm, inverse, scale):
    through = grad * (1.0 + scale)
    return inverse * (through - norm * jnp.mean(through * norm, axis=-1, keepdims=True))


def dot(left, right, contract, precision=None):
    return lax.dot_general(
        left, right, ((contract[:1], contract[1:]), ((), ())),
        precision=precision, preferred_element_type=F32,
    )


def sigma(v):
    return jax.nn.sigmoid(v)


def shards(
    latent, noise, timesteps, condition, embed_weight, embed_bias, modulation, modulation_bias,
    project_in, project_out, gate_up, down_weight, final_modulation, final_offsets, final_weight,
    final_bias, cotangent,
):
    highest = lax.Precision.HIGHEST
    images, height, across, chans = latent.shape
    width = condition.shape[-1]
    head = width // HEADS
    own_heads = HEADS // RANKS
    share = own_heads * head
    factor = 1.0 / math.sqrt(head)
    feed = gate_up.shape[-1] // 2
    feed_share = feed // RANKS
    high = modulation.shape[0]
    group = lax.axis_index("h")
    half = lax.axis_index("x")
    rank = rank_of()

    lanes = 128
    narrow = -(-3 * share // 128) * 128
    in_cols = project_in.reshape(high, 3, RANKS, share).transpose(2, 0, 1, 3)
    in_cols = jnp.pad(in_cols.reshape(RANKS, high, -1), ((0, 0), (0, 0), (0, narrow - 3 * share)))
    mods, cond_all, cond_own, mod_weight, gate_weight, in_narrow, out_weight, down_share = start(
        modulation, final_modulation, gate_up, in_cols, project_out, down_weight,
        condition.reshape(images, -1, width),
    )
    out_weight = out_weight.reshape(-1, width)
    down_share = down_share.reshape(-1, width)

    times = (timesteps.astype(F32) / 1000.0)[:, None, None, None]
    noisy = (1.0 - times) * latent + times * noise
    tiles = jnp.concatenate([noisy, cotangent], 3)
    tiles = jnp.concatenate([shifted(tiles[:, -1:], ("h", "l"), 1), tiles[:, :-1]], 1)
    tiles = jnp.concatenate([shifted(tiles[:, :, -1:], ("gx",), 1), tiles[:, :, :-1]], 2)
    flat = jnp.concatenate([unfold(tiles[..., :chans]), unfold(tiles[..., chans:])], 2)
    flat = swapped(flat, group).reshape(-1, 2 * PATCH * PATCH * chans)
    patches, grad_rows = jnp.split(flat, 2, axis=1)
    cond = cond_own.reshape(-1, width).astype(F32)
    cond_sigma = sigma(cond)
    own_shape, all_shape = (cond.shape[0], width), (RANKS, cond.shape[0], width)
    tokens = RANKS * cond.shape[0]

    def every(columns, kind):
        return ((RANKS, cond.shape[0], columns), kind)

    embedded = dot(patches, embed_weight, (1, 0), highest) + embed_bias
    bias = jnp.concatenate([modulation_bias, final_offsets]).reshape(RANKS, 1, width)
    shift_a, scale_a, gate_a, shift_b, scale_b, gate_b, shift_f, scale_f = mods.astype(F32) + bias
    norm_a, inv_a = normed(embedded)
    attend_in = (norm_a * (1.0 + scale_a) + shift_a).astype(BF16)
    branch, attend_all, qkv, mixed, in_weight = segment(
        functools.partial(attend_kernel, factor, head), 5, (attend_in, in_narrow, out_weight),
        [(own_shape, F32), (all_shape, BF16), every(6 * lanes, BF16), every(2 * lanes, BF16),
         ((width, 6 * lanes), BF16)],
        [], own_shape,
    )
    h_one = embedded + gate_a * branch
    norm_b, inv_b = normed(h_one)
    ffn_in = (norm_b * (1.0 + scale_b) + shift_b).astype(BF16)
    ffn, ffn_all, gateup = segment(
        feed_kernel, 6, (ffn_in, gate_weight, down_share),
        [(own_shape, F32), (all_shape, BF16), every(2 * feed_share, F32)], [], own_shape,
    )
    h_two = h_one + gate_b * ffn
    norm_f, inv_f = normed(h_two)
    final_in = norm_f * (1.0 + scale_f) + shift_f
    rows_out = dot(final_in, final_weight, (1, 0), highest) + final_bias

    final_bias_grad = jnp.sum(grad_rows, axis=0)
    final_weight_grad = dot(grad_rows, final_in, (0, 0), highest)
    grad_final_in = dot(grad_rows, final_weight, (1, 1), highest)
    grad_h_two = modnorm_back(grad_final_in, norm_f, inv_f, scale_f)
    grad_shift_f, grad_scale_f = grad_final_in, grad_final_in * norm_f
    grad_gate_b = grad_h_two * ffn
    grad_ffn_in, gate_grad, down_grad = segment(
        feed_back_kernel, 7,
        ((grad_h_two * gate_b).astype(BF16), gate_weight, down_share, gateup, ffn_all),
        [(own_shape, F32), (gate_weight.shape, BF16), (down_share.shape, BF16)],
        [(all_shape, BF16), every(2 * feed_share, BF16), every(feed_share, BF16)], own_shape,
    )
    grad_h_one = grad_h_two + modnorm_back(grad_ffn_in, norm_b, inv_b, scale_b)
    grad_shift_b, grad_scale_b = grad_ffn_in, grad_ffn_in * norm_b
    grad_gate_a = grad_h_one * branch
    grad_attend, in_grad, out_grad, gate_land, down_land = segment(
        functools.partial(attend_back_kernel, factor, head), 8,
        ((grad_h_one * gate_a).astype(BF16), in_weight, out_weight, attend_all, qkv, mixed,
         gate_grad, down_grad),
        [(own_shape, F32), (in_narrow.shape, BF16), (out_weight.shape, BF16),
         ((RANKS, high, 2 * feed_share), BF16), ((feed_share // 2, width), BF16)],
        [(all_shape, BF16), every(2 * lanes, BF16), every(6 * lanes, BF16),
         ((2, tokens, lanes), F32), ((2, tokens, lanes), F32)], own_shape, True,
    )
    grad_embedded = grad_h_one + modnorm_back(grad_attend, norm_a, inv_a, scale_a)
    grad_shift_a, grad_scale_a = grad_attend, grad_attend * norm_a
    grad_mods = jnp.stack(
        [grad_shift_a, grad_scale_a, grad_gate_a, grad_shift_b, grad_scale_b, grad_gate_b,
         grad_shift_f, grad_scale_f]
    )
    grad_cond, mod_grad, in_land, out_land = segment(
        mod_back_kernel, 9, (grad_mods.astype(BF16), mod_weight, cond_all, in_grad, out_grad),
        [(own_shape, F32), (mod_weight.shape, BF16), ((RANKS, high, narrow), BF16),
         ((high, width), BF16)], [(all_shape, BF16)], own_shape, True,
    )
    grad_cond = grad_cond * cond_sigma * (1.0 + cond * (1.0 - cond_sigma))
    grad_cond = swapped(grad_cond.astype(BF16).reshape(images, -1, width), group)
    condition_grad = grad_cond.astype(F32).reshape(condition.shape)

    embed_weight_grad = dot(patches, grad_embedded, (0, 0), highest)
    grad_patches = dot(grad_embedded, embed_weight, (1, 1), highest)
    small = jnp.concatenate(
        [
            jnp.sum(grad_mods, axis=1),
            jnp.sum(grad_embedded, axis=0, keepdims=True),
            embed_weight_grad,
            final_weight_grad,
            jnp.pad(final_bias_grad, (0, width - final_bias_grad.shape[0]))[None],
        ],
        0,
    )
    count = small.size
    part = -(-count // (PLACES * 1024)) * 1024
    small = jnp.pad(small.reshape(-1), (0, PLACES * part - count)).reshape(PLACES, 8, -1)
    mods_out, gates_out, ins_out, down_out, out_out, small = finish(
        mod_grad, gate_grad, gate_land, in_grad, in_land, down_grad, down_land, out_grad, out_land, small
    )

    def images_sum(value):
        value = value.astype(F32)
        return lax.psum(value, "ih") if lax.axis_size("ih") > 1 else value

    small = images_sum(small).reshape(-1)[:count].reshape(-1, width)
    mod_bias_grad = small[:6].reshape(-1)
    offsets_grad = small[6:8].reshape(-1)
    embed_bias_grad = small[8]
    patch = PATCH * PATCH * chans
    embed_weight_grad = small[9 : 9 + patch]
    final_weight_grad = small[9 + patch : 9 + 2 * patch].T
    final_bias_grad = small[9 + 2 * patch, :patch]

    flat = jnp.concatenate([rows_out, grad_patches], 1).reshape(images, -1, 2 * patch)
    flat = swapped(flat, group)
    tiles = jnp.concatenate(
        [refold(flat[..., :patch], images, height, across, chans),
         refold(flat[..., patch:], images, height, across, chans)], 3)
    tiles = jnp.concatenate([tiles[:, 1:], shifted(tiles[:, :1], ("h", "l"), -1)], 1)
    tiles = jnp.concatenate([tiles[:, :, 1:], shifted(tiles[:, :, :1], ("gx",), -1)], 2)
    prediction = tiles[..., :chans]
    latent_grad = (1.0 - times) * tiles[..., chans:]

    mods_out, gate_up_grad = images_sum(mods_out), images_sum(gates_out)
    gate_up_grad = gate_up_grad.reshape(high, RANKS, 2, feed_share).transpose(0, 2, 1, 3)
    project_in_grad = images_sum(ins_out)[..., : 3 * share].reshape(RANKS, high, 3, share)
    project_in_grad = project_in_grad.transpose(1, 2, 0, 3).reshape(high, -1)
    return (
        prediction,
        latent_grad,
        condition_grad,
        embed_weight_grad,
        embed_bias_grad,
        mods_out[:, : 6 * width],
        mod_bias_grad,
        project_in_grad,
        images_sum(out_out),
        gate_up_grad.reshape(high, -1),
        images_sum(down_out),
        mods_out[:, 6 * width :],
        offsets_grad,
        final_weight_grad,
        final_bias_grad,
    )


def solution(mesh):
    pairs = mesh.shape["img"] // 2
    split = Mesh(
        mesh.devices.reshape(pairs, 2, 2, mesh.shape["gy"] // 2, mesh.shape["gx"]),
        ("ih", "x", "h", "l", "gx"),
    )
    img, gy, gx = ("ih", "x"), ("h", "l"), "gx"
    tiles = P(img, gy, gx, None)
    held = P(("h", "l", "gx"), None)
    in_specs = (
        tiles, tiles, P(img), tiles, P(), P(), held, P(), held, held, held, held, held, P(), P(), P(), tiles,
    )
    out_specs = (
        tiles, tiles, tiles, P(), P(), held, P(), held, held, held, held, held, P(), P(), P(),
    )
    return jax.shard_map(shards, mesh=split, in_specs=in_specs, out_specs=out_specs, check_vma=False)
```
